32 devices in a mesh: section: 8 (over z, y), rep: 4 (over x, core).
Axes of the slice: x: 2, y: 2, z: 4, core: 2. Of those that a mesh axis runs over, the one named last changes fastest.
Arguments:
- document_token_embedding: bfloat16 [8, 128, 4096], P('rep'), may hold values from -6 to 6
- doc_lengths: int32 [8, 4], P('rep'), may hold values from 1 to 32, as said below
- docid_embed: bfloat16 [8, 32, 4096], P('rep'), may hold values from -6 to 6
- docid_targets: int32 [8, 32], P('rep'), may hold values from 0 to 16383
- enc_gain: float32 [5, 4096], replicated, may hold values from 0.1 to 1.9
- dec_gain: float32 [2, 4096], replicated, may hold values from 0.1 to 1.9
- w_enc_qkv: bfloat16 [3, 12288, 4096], P(None, 'section'), may hold values from -0.03125 to 0.03125
- w_enc_out: bfloat16 [12288, 4096], P('section'), may hold values from -0.75 to 0.75
- cross_query_key_value_weight: bfloat16 [3, 4096, 4096], P(None, 'section'), may hold values from -0.03125 to 0.03125
- w_cross_out: bfloat16 [4096, 4096], P('section'), may hold values from -0.75 to 0.75
- docid_head_weight: bfloat16 [4096, 16384], P(None, 'section'), may hold values from -0.25 to 0.25
Outputs:
- logits: bfloat16 [8, 32, 16384], P('rep', None, 'section')
- token_loss: float32 [8, 32], P('rep')
- mean_loss: float32 [], replicated
The draws below stay inside these ranges and needn't reach their ends.
Inputs may be any that keep to these rules, and one draw needn't show every extreme that they name: `doc_lengths`: in every draw some document has exactly 32 tokens.
All inputs are finite; a program needn't handle non-finite values.
Results may differ from the reference program's by a relative error of at most 0.019.
Values may be sent and summed in bfloat16 or wider, within the bound.
A program may use at most 128 MiB of HBM per device.

```python
import jax
import jax.numpy as jnp
from jax import lax

D = 4096
HD = 64
XHEADS = 64
HEADS = 48
VOCAB = 16384
GROUPS = 4
DOCS = 4
DLEN = 8
LMAX = 32
ROWS = 128
DROWS = 32
BATCH = 8


def draw_doc_lengths(key, part):
    key_left, key_right, key_pick = jax.random.split(jax.random.fold_in(key, 17), 3)
    left_draw = jax.random.randint(key_left, (BATCH, DOCS), 0, LMAX)
    right_draw = jax.random.randint(key_right, (BATCH, DOCS), 0, LMAX)
    lengths = 1 + left_draw * right_draw // LMAX
    chosen = jax.random.randint(key_pick, (), 0, BATCH * DOCS)
    flattened = jnp.where(jnp.arange(BATCH * DOCS) == chosen, LMAX, lengths.reshape(-1))
    return flattened.reshape(BATCH, DOCS).astype(jnp.int32)


def touch_ends(array, stream_key, low, top_value):
    extent = array.shape
    place = [jax.random.randint(jax.random.fold_in(stream_key, axis), (), 0, extent[axis]) for axis in range(len(extent))]
    array = array.at[tuple(place)].set(low)
    longest = extent.index(max(extent))
    place[longest] = (place[longest] + 1) % extent[longest]
    return array.at[tuple(place)].set(top_value)


def block_levels(rng, shape, shards, low, top_value):
    def one(dim, shards_of):
        steps = jax.random.uniform(jax.random.fold_in(jax.random.fold_in(rng, 6), dim), (shards_of,), jnp.float32, low / len(shards), top_value / len(shards))
        return jnp.repeat(jnp.exp(steps), shape[dim] // shards_of).reshape((-1,) + (1,) * (len(shape) - dim - 1))

    level = one(*shards[0])
    for cut in shards[1:]:
        level = level * one(*cut)
    return level


def noise(own_key, extent, spread, reach, pieces=(), dtype=jnp.bfloat16):
    array = jax.random.normal(own_key, extent, jnp.float32) * spread
    if len(pieces) > 0:
        array = block_levels(own_key, extent, pieces, -0.22, 0.18) * array
    return jnp.clip(array, min=-reach, max=reach).astype(dtype)


def setup_inputs(seed: int = 0) -> dict:
    seeds = jax.random.split(jax.random.key(seed), 12)
    document_token_embedding = noise(seeds[0], (BATCH, ROWS, D), 1.0, 6.0, ((0, 4),))
    doc_lengths = draw_doc_lengths(jax.random.fold_in(seeds[11], 71), 0)
    docid_embed = noise(seeds[2], (BATCH, DROWS, D), 1.0, 6.0, ((0, 4),))
    docid_targets = touch_ends(jax.random.randint(seeds[3], (BATCH, DROWS), 0, VOCAB), jax.random.fold_in(seeds[3], 1), 0, VOCAB - 1).astype(jnp.int32)
    enc_gain = jnp.clip(1.0 + 0.18 * jax.random.normal(seeds[4], (GROUPS + 1, D), jnp.float32), 0.1, 1.9)
    dec_gain = jnp.clip(1.0 + 0.18 * jax.random.normal(seeds[5], (2, D), jnp.float32), 0.1, 1.9)
    w_enc_qkv = noise(seeds[6], (3, GROUPS * HEADS * HD, D), (D * 8) ** -0.5, 0.03125, ((1, 8),))
    w_enc_out = noise(seeds[7], (GROUPS * HEADS * HD, D), HD ** -0.5, 0.75, ((0, 8),))
    cross_query_key_value_weight = noise(seeds[8], (3, XHEADS * HD, D), (D * 8) ** -0.5, 0.03125, ((1, 8),))
    w_cross_out = noise(seeds[9], (XHEADS * HD, D), HD ** -0.5, 0.75, ((0, 8),))
    docid_head_weight = noise(seeds[10], (D, VOCAB), (D // 9) ** -0.5, 0.25, ((1, 8),))
    return {"document_token_embedding": document_token_embedding, "doc_lengths": doc_lengths, "docid_embed": docid_embed, "docid_targets": docid_targets, "enc_gain": enc_gain, "dec_gain": dec_gain, "w_enc_qkv": w_enc_qkv, "w_enc_out": w_enc_out, "cross_query_key_value_weight": cross_query_key_value_weight, "w_cross_out": w_cross_out, "docid_head_weight": docid_head_weight}


def norm_rows(values, gain):
    values = values.astype(jnp.float32)
    scale = lax.rsqrt(lax.optimization_barrier(jnp.mean(values * values, axis=-1, keepdims=True)) + 1e-06)
    return values * scale * gain

def attend(queries, key_rows, values, allowed):
    scores = jnp.einsum('qhe,khe->hqk', queries.astype(jnp.float32), key_rows.astype(jnp.float32))
    attention_weight_rows = jnp.where(allowed[None], jnp.exp(scores), 0.0)
    probabilities = (attention_weight_rows / lax.optimization_barrier(jnp.sum(attention_weight_rows, axis=-1, keepdims=True))).astype(jnp.bfloat16)
    mixture = jnp.einsum('hqk,khe->qhe', probabilities.astype(jnp.float32), values.astype(jnp.float32))
    return mixture.astype(jnp.bfloat16)

def project(normed, weight):
    return jnp.dot(normed, weight.T, preferred_element_type=jnp.float32).astype(jnp.bfloat16)

def reference(document_token_embedding, doc_lengths, docid_embed, docid_targets, enc_gain, dec_gain, w_enc_qkv, w_enc_out, cross_query_key_value_weight, w_cross_out, docid_head_weight):
    width_heads = HEADS * HD
    positions = jnp.arange(DOCS * LMAX)
    key_doc = positions // LMAX
    key_place = positions % LMAX
    decoder_doc = jnp.arange(DOCS * DLEN) // DLEN

    def per_sample(sample):
        doc_rows, lengths, docid_rows, targets = sample
        live_keys = key_place < lengths[key_doc]
        allowed = (key_doc[:, None] == key_doc[None, :]) & live_keys[None, :]
        hidden = doc_rows
        for depth in range(GROUPS):
            normed = norm_rows(hidden, enc_gain[depth]).astype(jnp.bfloat16)
            lower = depth * width_heads
            upper = lower + width_heads
            projected = [project(normed, w_enc_qkv[member, lower:upper]).reshape(-1, HEADS, HD) for member in range(3)]
            mixture = attend(projected[0], projected[1], projected[2], allowed).reshape(-1, width_heads)
            update = jnp.dot(mixture, w_enc_out[lower:upper], preferred_element_type=jnp.float32)
            hidden = (hidden.astype(jnp.float32) + update).astype(jnp.bfloat16)
        encoder_memory = norm_rows(hidden, enc_gain[GROUPS]).astype(jnp.bfloat16)
        dec_normed = norm_rows(docid_rows, dec_gain[0]).astype(jnp.bfloat16)
        queries = project(dec_normed, cross_query_key_value_weight[0]).reshape(-1, XHEADS, HD)
        key_rows = project(encoder_memory, cross_query_key_value_weight[1]).reshape(-1, XHEADS, HD)
        values = project(encoder_memory, cross_query_key_value_weight[2]).reshape(-1, XHEADS, HD)
        cross_allowed = (decoder_doc[:, None] == key_doc[None, :]) & live_keys[None, :]
        mixture = attend(queries, key_rows, values, cross_allowed).reshape(-1, XHEADS * HD)
        update = jnp.dot(mixture, w_cross_out, preferred_element_type=jnp.float32)
        closing_rows = norm_rows(docid_rows.astype(jnp.float32) + update, dec_gain[1]).astype(jnp.bfloat16)
        scores_vocab = jnp.dot(closing_rows, docid_head_weight, preferred_element_type=jnp.float32)
        totals = jnp.log(lax.optimization_barrier(jnp.sum(jnp.exp(scores_vocab), axis=-1)))
        picked = jnp.take_along_axis(scores_vocab, targets[:, None].astype(jnp.int32), axis=-1)[:, 0]
        return (scores_vocab.astype(jnp.bfloat16), totals - picked)
    logits, token_loss = lax.map(per_sample, (document_token_embedding, doc_lengths, docid_embed, docid_targets))
    return (logits, token_loss, jnp.mean(token_loss))
```

```python
import functools

import jax
import jax.numpy as jnp
from jax import lax
from jax.experimental import pallas as pl
from jax.experimental.pallas import tpu as pltpu
from jax.sharding import PartitionSpec as P

HD = 64
GROUPS = 4
WTILE = 512
PARTS = 4
MESH = pl.DeviceIdType.MESH


def from_partner(block, axis, distance):
    count = lax.axis_size(axis)
    route = []
    for low in range(count):
        high = low | 1 << distance
        if high != low and high < count:
            route += [(low, high), (high, low)]
    return lax.ppermute(block, axis, route)


def from_behind(block, axis, distance):
    devices = range(lax.axis_size(axis))
    route = [(i - distance, i) for i in devices if i - distance in devices]
    return lax.ppermute(block, axis, route)


def passed_along(shard, axis, by):
    size = lax.axis_size(axis)
    return lax.ppermute(shard, axis, [(i, (i + by) % size) for i in range(size)])


def norm_rows(values, gain):
    values = values.astype(jnp.float32)
    scale = lax.rsqrt(jnp.mean(values * values, axis=-1, keepdims=True) + 1e-06)
    return values * scale * gain


def attend(queries, key_rows, values, allowed):
    scores = jnp.einsum("qhe,khe->hqk", queries, key_rows, preferred_element_type=jnp.float32)
    attention_weight_rows = jnp.where(allowed[None], jnp.exp(scores), 0.0)
    probabilities = (
        attention_weight_rows / jnp.sum(attention_weight_rows, axis=-1, keepdims=True)
    ).astype(jnp.bfloat16)
    mixture = jnp.einsum("hqk,khe->qhe", probabilities, values, preferred_element_type=jnp.float32)
    return mixture.astype(jnp.bfloat16)


def live_keys(lengths, key_doc, key_place):
    owners = jnp.arange(lengths.shape[0])
    matches = (key_doc[:, None] == owners[None, :]) & (key_place[:, None] < lengths[None, :])
    return jnp.any(matches, axis=1)


def lane_gather(own_rows, lane_bits, lane_index, concat_dim):
    for bit_number in range(lane_bits):
        partner = from_partner(own_rows, "section", bit_number)
        lower_half = lane_index // (1 << bit_number) % 2 == 0
        own_rows = jnp.where(
            lower_half,
            jnp.concatenate([own_rows, partner], concat_dim),
            jnp.concatenate([partner, own_rows], concat_dim),
        )
    return own_rows


def lane_reduce(totals, lane_bits, lane_index):
    for bit_number in reversed(range(lane_bits)):
        half_rows = totals.shape[0] // 2
        lower_half = lane_index // (1 << bit_number) % 2 == 0
        kept_rows = jnp.where(lower_half, totals[:half_rows], totals[half_rows:])
        outgoing = jnp.where(lower_half, totals[half_rows:], totals[:half_rows])
        totals = kept_rows + from_partner(outgoing, "section", bit_number)
    return totals


def relay_memory(encoder_memory, group_index, lane_count):
    encoder_memory = jnp.where(group_index == 0, encoder_memory, jnp.zeros_like(encoder_memory))
    for stride in (1, 2):
        encoder_memory = encoder_memory + from_behind(
            encoder_memory, "section", stride * lane_count
        )
    return encoder_memory


def shards(
    document_token_embedding,
    doc_lengths,
    docid_embed,
    docid_targets,
    enc_gain,
    dec_gain,
    w_enc_qkv,
    w_enc_out,
    cross_query_key_value_weight,
    w_cross_out,
    docid_head_weight,
):
    lane_count = lax.axis_size("section") // GROUPS
    lane_bits = lane_count.bit_length() - 1
    section_index = lax.axis_index("section")
    group_index = section_index // lane_count
    lane_index = section_index % lane_count
    micro_count, row_count, model_width = document_token_embedding.shape
    doc_count = doc_lengths.shape[1]
    doc_span = row_count // doc_count
    block_rows = row_count // lane_count
    local_heads = w_enc_qkv.shape[1] // HD
    positions = jnp.arange(row_count)
    key_doc = positions // doc_span
    key_place = positions % doc_span
    same_doc = key_doc[:, None] == key_doc[None, :]

    def partial_update(normed, lengths):
        allowed = same_doc & live_keys(lengths, key_doc, key_place)[None, :]
        projected = jnp.einsum(
            "rd,mcd->mrc", normed, w_enc_qkv, preferred_element_type=jnp.float32
        ).astype(jnp.bfloat16)
        projected = projected.reshape(3, row_count, local_heads, HD)
        mixture = attend(projected[0], projected[1], projected[2], allowed).reshape(row_count, -1)
        return jnp.dot(mixture, w_enc_out, preferred_element_type=jnp.float32)

    def section_step(step_index, loop_state):
        handed, encoder_memory = loop_state
        micro_index = step_index - group_index
        slot_index = jnp.clip(micro_index, 0, micro_count - 1)
        lengths = lax.dynamic_index_in_dim(doc_lengths, slot_index, 0, keepdims=False)
        layer_gain = lax.dynamic_index_in_dim(enc_gain, group_index, 0, keepdims=False)
        incoming = lax.dynamic_index_in_dim(
            document_token_embedding, jnp.minimum(step_index, micro_count - 1), 0, keepdims=False
        )
        incoming = lax.dynamic_slice_in_dim(incoming, lane_index * block_rows, block_rows, 0)
        current = jnp.where(group_index == 0, incoming, handed)
        normed = lane_gather(
            norm_rows(current, layer_gain).astype(jnp.bfloat16), lane_bits, lane_index, 0
        )
        summed = lane_reduce(partial_update(normed, lengths), lane_bits, lane_index)
        result = (current.astype(jnp.float32) + summed).astype(jnp.bfloat16)
        handed = passed_along(result, "section", lane_count)
        finished_index = step_index - (GROUPS - 1)
        finished_slot = jnp.clip(finished_index, 0, micro_count - 1)
        keeping = (group_index == 0) & (finished_index >= 0) & (finished_index < micro_count)
        stored = lax.dynamic_update_index_in_dim(encoder_memory, handed, finished_slot, 0)
        encoder_memory = jnp.where(keeping, stored, encoder_memory)
        return (handed, encoder_memory)

    handed = jnp.zeros((block_rows, model_width), jnp.bfloat16)
    encoder_memory = jnp.zeros((micro_count, block_rows, model_width), jnp.bfloat16)
    handed, encoder_memory = lax.fori_loop(
        0, micro_count + GROUPS - 1, section_step, (handed, encoder_memory)
    )
    encoder_memory = norm_rows(encoder_memory, enc_gain[GROUPS]).astype(jnp.bfloat16)
    encoder_memory = relay_memory(encoder_memory, group_index, lane_count)
    encoder_memory = lane_gather(encoder_memory, lane_bits, lane_index, 1)
    decoder_rows = docid_embed.shape[1]
    docid_span = decoder_rows // doc_count
    decoder_doc = jnp.arange(decoder_rows) // docid_span
    cross_heads = cross_query_key_value_weight.shape[1] // HD
    dec_normed = norm_rows(docid_embed, dec_gain[0]).astype(jnp.bfloat16)
    queries = jnp.einsum(
        "brd,cd->brc",
        dec_normed,
        cross_query_key_value_weight[0],
        preferred_element_type=jnp.float32,
    ).astype(jnp.bfloat16)
    memory_heads = jnp.einsum(
        "pye,qve->qpyv",
        encoder_memory,
        cross_query_key_value_weight[1:],
        preferred_element_type=jnp.float32,
    ).astype(jnp.bfloat16)

    def cross_one(sample_queries, sample_keys, sample_values, lengths):
        allowed = (decoder_doc[:, None] == key_doc[None, :]) & live_keys(
            lengths, key_doc, key_place
        )[None, :]
        return attend(sample_queries, sample_keys, sample_values, allowed)

    mixture = jax.vmap(cross_one)(
        queries.reshape(micro_count, decoder_rows, cross_heads, HD),
        memory_heads[0].reshape(micro_count, row_count, cross_heads, HD),
        memory_heads[1].reshape(micro_count, row_count, cross_heads, HD),
        doc_lengths,
    )
    cross_terms = jnp.einsum(
        "brc,cd->brd",
        mixture.reshape(micro_count, decoder_rows, -1),
        w_cross_out,
        preferred_element_type=jnp.float32,
    )
    cross_sum = lax.psum(cross_terms, "section")
    closing_rows = norm_rows(docid_embed.astype(jnp.float32) + cross_sum, dec_gain[1]).astype(
        jnp.bfloat16
    )
    scores_vocab = jnp.einsum(
        "brd,dv->brv", closing_rows, docid_head_weight, preferred_element_type=jnp.float32
    )
    vocab_local = docid_head_weight.shape[1]
    vocab_start = section_index * vocab_local
    matches = docid_targets[..., None] == vocab_start + jnp.arange(vocab_local)
    exponent_total, picked = lax.psum(
        (
            jnp.sum(jnp.exp(scores_vocab), axis=-1),
            jnp.sum(jnp.where(matches, scores_vocab, 0.0), axis=-1),
        ),
        "section",
    )
    token_loss = jnp.log(exponent_total) - picked
    mean_loss = lax.psum(jnp.sum(token_loss), "rep") / (token_loss.size * lax.axis_size("rep"))
    return (scores_vocab.astype(jnp.bfloat16), token_loss, mean_loss)


def encoder_kernel(
    sent,
    x_ref,
    gain_ref,
    row_doc_ref,
    key_doc_ref,
    wqkv_ref,
    wout_ref,
    mem_ref,
    wqkv_v,
    wout_v,
    hid,
    work,
    part,
    qkv,
    mix,
    w_sem,
    o_sem,
    x_sem,
    gs,
    gr,
    rs,
    rr,
    zs,
    zr,
    bs,
    br,
    ms,
    mr,
):
    rows, width = hid.shape
    half = sent // 2
    columns = width // PARTS
    tiles = wqkv_v.shape[0]
    per = tiles // 3
    section = lax.axis_index("section")
    count = lax.axis_size("section")
    group = section // 2
    lane = section % 2
    partner = section + 1 - 2 * lane
    ahead = lax.rem(section + 2, count)
    behind = lax.rem(section + count - 2, count)
    own = pl.ds(pl.multiple_of(lane * half, 16), half)
    other = pl.ds(pl.multiple_of((1 - lane) * half, 16), half)

    def cols(c):
        return pl.ds(pl.multiple_of(c * columns, columns), columns)

    def weight_copy(j):
        return pltpu.make_async_copy(
            wqkv_ref.at[j // per, pl.ds((j % per) * WTILE, WTILE)], wqkv_v.at[j], w_sem.at[j]
        )

    def out_copy(c):
        return pltpu.make_async_copy(wout_ref.at[:, cols(c)], wout_v.at[c], o_sem.at[c])

    def remote(src, dst, send, recv, device):
        return pltpu.make_async_remote_copy(
            src_ref=src,
            dst_ref=dst,
            send_sem=send,
            recv_sem=recv,
            device_id={"section": device},
            device_id_type=MESH,
        )

    def gather(c, block):
        return remote(hid.at[block, cols(c)], hid.at[block, cols(c)], gs.at[c], gr.at[c], partner)

    def reduce(c):
        return remote(work.at[other, cols(c)], part.at[:, cols(c)], rs.at[c], rr.at[c], partner)

    def hand(c):
        return remote(hid.at[own, cols(c)], hid.at[own, cols(c)], zs.at[c], zr.at[c], ahead)

    def back(c):
        return remote(mem_ref.at[own, cols(c)], mem_ref.at[own, cols(c)], bs.at[c], br.at[c], behind)

    def spread(c, block):
        return remote(
            mem_ref.at[block, cols(c)], mem_ref.at[block, cols(c)], ms.at[c], mr.at[c], partner
        )

    def each(size, body):
        def step(i, carry):
            body(i)
            return carry

        lax.fori_loop(0, size, step, 0)

    entry = pltpu.make_async_copy(x_ref.at[pl.ds(0, sent)], hid.at[pl.ds(0, sent)], x_sem)

    @pl.when(group == 0)
    def _():
        entry.start()

    for j in range(tiles):
        weight_copy(j).start()
    for c in range(PARTS):
        out_copy(c).start()

    barrier = pltpu.get_barrier_semaphore()
    for device in (partner, ahead, behind):
        pl.semaphore_signal(barrier, inc=1, device_id={"section": device}, device_id_type=MESH)
    pl.semaphore_wait(barrier, 3)

    if sent < rows:
        hid[sent:, :] = jnp.zeros((rows - sent, width), hid.dtype)
    if sent < mem_ref.shape[0]:
        mem_ref[sent:, :] = jnp.zeros((mem_ref.shape[0] - sent, width), mem_ref.dtype)

    @pl.when(group == 0)
    def _():
        entry.wait()

    @pl.when(group > 0)
    def _():
        def arrive(c):
            hand(c).wait_recv()
            gather(c, own).start()

        each(PARTS, arrive)

        def complete(c):
            gather(c, other).wait_recv()
            gather(c, own).wait_send()

        each(PARTS, complete)

    def norm(r):
        block = pl.ds(pl.multiple_of(r * 16, 16), 16)
        values = hid[block, :].astype(jnp.float32)
        scale = lax.rsqrt(jnp.mean(values * values, axis=-1, keepdims=True) + 1e-06)
        work[block, :] = (values * scale * gain_ref[...]).astype(work.dtype)

    each(rows // 16, norm)

    def project(j):
        pltpu.make_async_copy(
            wqkv_ref.at[0, pl.ds(0, WTILE)], wqkv_v.at[j], w_sem.at[j]
        ).wait()
        qkv[j] = lax.dot_general(
            work[...], wqkv_v[j], (((1,), (1,)), ((), ())), preferred_element_type=jnp.float32
        ).astype(qkv.dtype)

    each(tiles, project)
    pairs = WTILE // (2 * HD)

    def attend_pair(p):
        tile = p // pairs
        span = pl.ds(pl.multiple_of((p % pairs) * 2 * HD, 2 * HD), 2 * HD)
        queries = qkv[tile, :, span]
        keys = qkv[per + tile, :, span]
        values = qkv[2 * per + tile, :, span]
        allowed = row_doc_ref[...] == key_doc_ref[...]
        first = lax.broadcasted_iota(jnp.int32, (rows, 2 * HD), 1) < HD
        mixed = []
        for side in range(2):
            keep = first if side == 0 else jnp.logical_not(first)
            chosen = jnp.where(keep, queries.astype(jnp.float32), 0.0).astype(jnp.bfloat16)
            scores = lax.dot_general(
                chosen, keys, (((1,), (1,)), ((), ())), preferred_element_type=jnp.float32
            )
            weights = jnp.where(allowed, jnp.exp(scores), 0.0)
            shares = (weights / jnp.sum(weights, axis=-1, keepdims=True)).astype(jnp.bfloat16)
            mixed.append(jnp.dot(shares, values, preferred_element_type=jnp.float32))
        mix[:, pl.ds(pl.multiple_of(p * 2 * HD, 2 * HD), 2 * HD)] = jnp.where(
            first, mixed[0], mixed[1]
        ).astype(mix.dtype)

    each(per * pairs, attend_pair)

    def output(c):
        out_copy(c).wait()
        work[:, cols(c)] = jnp.dot(
            mix[...], wout_v[c], preferred_element_type=jnp.float32
        ).astype(work.dtype)
        reduce(c).start()

    each(PARTS, output)

    def total(c):
        reduce(c).wait_recv()
        return (
            hid[own, cols(c)].astype(jnp.float32)
            + work[own, cols(c)].astype(jnp.float32)
            + part[:, cols(c)].astype(jnp.float32)
        ).astype(hid.dtype)

    @pl.when(group < GROUPS - 1)
    def _():
        def finish(c):
            hid[own, cols(c)] = total(c)
            hand(c).start()

        each(PARTS, finish)

        def relay(c):
            back(c).wait_recv()

            @pl.when(group > 0)
            def _():
                back(c).start()

            spread(c, own).start()

        each(PARTS, relay)

    @pl.when(group == GROUPS - 1)
    def _():
        def finish(c):
            mem_ref[own, cols(c)] = total(c)
            back(c).start()
            spread(c, own).start()

        each(PARTS, finish)

    def drain(c):
        spread(c, other).wait_recv()
        spread(c, own).wait_send()
        reduce(c).wait_send()

        @pl.when(group < GROUPS - 1)
        def _():
            hand(c).wait_send()

        @pl.when(group > 0)
        def _():
            back(c).wait_send()

    each(PARTS, drain)


def encode(rows, sent, number, x, gain, row_doc, key_doc, wqkv, wout):
    total_rows, width = x.shape
    inner = wout.shape[0]
    tiles = 3 * (inner // WTILE)
    dma = pltpu.SemaphoreType.DMA
    vmem = pl.BlockSpec(memory_space=pltpu.VMEM)
    anywhere = pl.BlockSpec(memory_space=pl.ANY)
    return pl.pallas_call(
        functools.partial(encoder_kernel, sent),
        out_shape=jax.ShapeDtypeStruct((total_rows, width), jnp.bfloat16),
        in_specs=[anywhere, vmem, vmem, vmem, anywhere, anywhere],
        out_specs=vmem,
        scratch_shapes=[
            pltpu.VMEM((tiles, WTILE, width), jnp.bfloat16),
            pltpu.VMEM((PARTS, inner, width // PARTS), jnp.bfloat16),
            pltpu.VMEM((rows, width), jnp.bfloat16),
            pltpu.VMEM((rows, width), jnp.bfloat16),
            pltpu.VMEM((sent // 2, width), jnp.bfloat16),
            pltpu.VMEM((tiles, rows, WTILE), jnp.bfloat16),
            pltpu.VMEM((rows, inner), jnp.bfloat16),
            dma((tiles,)),
            dma((PARTS,)),
            dma,
        ]
        + [dma((PARTS,))] * 10,
        compiler_params=pltpu.CompilerParams(
            collective_id=number, has_side_effects=True, vmem_limit_bytes=67043328
        ),
        name=f"encoder_{sent}",
    )(x, gain, row_doc[:rows, None], key_doc[None, :rows], wqkv, wout)


def butterfly(value, axis, combine):
    for bit in range(lax.axis_size(axis).bit_length() - 1):
        value = combine(value, from_partner(value, axis, bit))
    return value


def halves_reduced(totals, bits, index):
    for bit in bits:
        half = totals.shape[0] // 2
        lower = index // (1 << bit) % 2 == 0
        kept = jnp.where(lower, totals[:half], totals[half:])
        outgoing = jnp.where(lower, totals[half:], totals[:half]).astype(jnp.bfloat16)
        totals = kept + from_partner(outgoing, "section", bit).astype(jnp.float32)
    return totals


def halves_gathered(rows, bits, index):
    for bit in bits:
        partner = from_partner(rows, "section", bit)
        lower = index // (1 << bit) % 2 == 0
        rows = jnp.where(
            lower, jnp.concatenate([rows, partner], 0), jnp.concatenate([partner, rows], 0)
        )
    return rows


def own_rows(rows, bits, index):
    for bit in bits:
        half = rows.shape[0] // 2
        lower = index // (1 << bit) % 2 == 0
        rows = jnp.where(lower, rows[:half], rows[half:])
    return rows


def fast_shards(
    document_token_embedding,
    doc_lengths,
    docid_embed,
    docid_targets,
    enc_gain,
    dec_gain,
    w_enc_qkv,
    w_enc_out,
    cross_query_key_value_weight,
    w_cross_out,
    docid_head_weight,
):
    section_index = lax.axis_index("section")
    group_index = section_index // 2
    micro_count, row_count, width = document_token_embedding.shape
    doc_count = doc_lengths.shape[1]
    doc_span = row_count // doc_count
    all_rows = micro_count * row_count
    positions = jnp.arange(all_rows)
    lengths = doc_lengths.reshape(-1)
    live = (jnp.arange(doc_span)[None, :] < lengths[:, None]).reshape(-1)
    ends = jnp.cumsum(lengths)
    live_count = ends[-1]
    starts = jnp.concatenate([jnp.zeros((1,), ends.dtype), ends[:-1]])
    inside = (positions[:, None] >= starts[None, :]) & (positions[:, None] < ends[None, :])
    docs = jnp.arange(lengths.shape[0])
    row_doc = jnp.sum(jnp.where(inside, docs[None, :], 0), axis=1).astype(jnp.int32)
    key_doc = jnp.where(positions < live_count, row_doc, -1).astype(jnp.int32)
    source = jnp.sum(
        jnp.where(inside, docs[None, :] * doc_span + positions[:, None] - starts[None, :], 0), axis=1
    )
    source = jnp.where(positions < live_count, source, -1)
    pick = (source[:, None] == positions[None, :]).astype(jnp.bfloat16)
    packed = jnp.dot(
        pick,
        document_token_embedding.reshape(all_rows, width),
        preferred_element_type=jnp.float32,
    ).astype(jnp.bfloat16)
    largest = butterfly(live_count.astype(jnp.float32)[None], "rep", jnp.maximum)[0]
    gain = lax.dynamic_slice_in_dim(enc_gain, group_index, 1, 0)
    unit = all_rows // 2
    sizes = [(unit, unit * 3 // 4), (unit, unit), (all_rows, all_rows)]
    choice = jnp.sum(jnp.stack([(largest > sent).astype(jnp.int32) for _, sent in sizes[:-1]]))
    branches = [
        functools.partial(encode, rows, sent, number) for number, (rows, sent) in enumerate(sizes)
    ]
    hidden = lax.switch(
        choice, branches, packed, gain, row_doc, key_doc, w_enc_qkv, w_enc_out
    )
    memory = norm_rows(hidden, enc_gain[GROUPS]).astype(jnp.bfloat16)

    decoder_rows = docid_embed.shape[1]
    every = micro_count * decoder_rows
    docid_span = decoder_rows // doc_count
    decoder_doc = jnp.arange(every) // docid_span
    cross_heads = cross_query_key_value_weight.shape[1] // HD
    flat_docid = docid_embed.reshape(every, width)
    dec_normed = norm_rows(flat_docid, dec_gain[0]).astype(jnp.bfloat16)

    def project(values, weight):
        return (
            jnp.einsum("rd,cd->rc", values, weight, preferred_element_type=jnp.float32)
            .astype(jnp.bfloat16)
            .reshape(-1, cross_heads, HD)
        )

    queries = project(dec_normed, cross_query_key_value_weight[0])
    keys = project(memory, cross_query_key_value_weight[1])
    values = project(memory, cross_query_key_value_weight[2])
    allowed = decoder_doc[:, None] == key_doc[None, :]
    mixture = attend(queries, keys, values, allowed).reshape(every, -1)
    cross_terms = jnp.dot(mixture, w_cross_out, preferred_element_type=jnp.float32)
    bits = range(lax.axis_size("section").bit_length() - 1)
    summed = halves_reduced(cross_terms, bits, section_index)
    residual = own_rows(flat_docid, bits, section_index).astype(jnp.float32)
    closing = norm_rows(residual + summed, dec_gain[1]).astype(jnp.bfloat16)
    closing = halves_gathered(closing, reversed(bits), section_index)
    scores_vocab = jnp.dot(closing, docid_head_weight, preferred_element_type=jnp.float32)
    vocab_local = docid_head_weight.shape[1]
    targets = docid_targets.reshape(-1)
    matches = targets[:, None] == section_index * vocab_local + jnp.arange(vocab_local)
    sums = jnp.stack(
        [
            jnp.sum(jnp.exp(scores_vocab), axis=-1),
            jnp.sum(jnp.where(matches, scores_vocab, 0.0), axis=-1),
        ]
    )
    sums = butterfly(sums, "section", jnp.add)
    token_loss = jnp.log(sums[0]) - sums[1]
    loss_sum = butterfly(jnp.sum(token_loss)[None], "rep", jnp.add)[0]
    mean_loss = loss_sum / (token_loss.size * lax.axis_size("rep"))
    logits = scores_vocab.astype(jnp.bfloat16).reshape(micro_count, decoder_rows, vocab_local)
    return (logits, token_loss.reshape(docid_targets.shape), mean_loss)


def solution(mesh):
    in_specs = (
        P("rep", None, None),
        P("rep", None),
        P("rep", None, None),
        P("rep", None),
        P(),
        P(),
        P(None, "section", None),
        P("section", None),
        P(None, "section", None),
        P("section", None),
        P(None, "section"),
    )
    out_specs = (P("rep", None, "section"), P("rep", None), P())
    local = shards if mesh.shape["section"] != 2 * GROUPS else fast_shards
    return jax.shard_map(local, mesh=mesh, in_specs=in_specs, out_specs=out_specs, check_vma=False)
```

```python
import functools

import jax
import jax.numpy as jnp
from jax import lax
from jax.experimental import pallas as pl
from jax.experimental.pallas import tpu as pltpu
from jax.sharding import PartitionSpec as P

HD = 64
GROUPS = 4
WTILE = 512
PARTS = 4
MESH = pl.DeviceIdType.MESH


def from_partner(block, axis, distance):
    count = lax.axis_size(axis)
    route = []
    for low in range(count):
        high = low | 1 << distance
        if high != low and high < count:
            route += [(low, high), (high, low)]
    return lax.ppermute(block, axis, route)


def from_behind(block, axis, distance):
    devices = range(lax.axis_size(axis))
    route = [(i - distance, i) for i in devices if i - distance in devices]
    return lax.ppermute(block, axis, route)


def passed_along(shard, axis, by):
    size = lax.axis_size(axis)
    return lax.ppermute(shard, axis, [(i, (i + by) % size) for i in range(size)])


def norm_rows(values, gain):
    values = values.astype(jnp.float32)
    scale = lax.rsqrt(jnp.mean(values * values, axis=-1, keepdims=True) + 1e-06)
    return values * scale * gain


def attend(queries, key_rows, values, allowed):
    scores = jnp.einsum("qhe,khe->hqk", queries, key_rows, preferred_element_type=jnp.float32)
    attention_weight_rows = jnp.where(allowed[None], jnp.exp(scores), 0.0)
    probabilities = (
        attention_weight_rows / jnp.sum(attention_weight_rows, axis=-1, keepdims=True)
    ).astype(jnp.bfloat16)
    mixture = jnp.einsum("hqk,khe->qhe", probabilities, values, preferred_element_type=jnp.float32)
    return mixture.astype(jnp.bfloat16)


def live_keys(lengths, key_doc, key_place):
    owners = jnp.arange(lengths.shape[0])
    matches = (key_doc[:, None] == owners[None, :]) & (key_place[:, None] < lengths[None, :])
    return jnp.any(matches, axis=1)


def lane_gather(own_rows, lane_bits, lane_index, concat_dim):
    for bit_number in range(lane_bits):
        partner = from_partner(own_rows, "section", bit_number)
        lower_half = lane_index // (1 << bit_number) % 2 == 0
        own_rows = jnp.where(
            lower_half,
            jnp.concatenate([own_rows, partner], concat_dim),
            jnp.concatenate([partner, own_rows], concat_dim),
        )
    return own_rows


def lane_reduce(totals, lane_bits, lane_index):
    for bit_number in reversed(range(lane_bits)):
        half_rows = totals.shape[0] // 2
        lower_half = lane_index // (1 << bit_number) % 2 == 0
        kept_rows = jnp.where(lower_half, totals[:half_rows], totals[half_rows:])
        outgoing = jnp.where(lower_half, totals[half_rows:], totals[:half_rows])
        totals = kept_rows + from_partner(outgoing, "section", bit_number)
    return totals


def relay_memory(encoder_memory, group_index, lane_count):
    encoder_memory = jnp.where(group_index == 0, encoder_memory, jnp.zeros_like(encoder_memory))
    for stride in (1, 2):
        encoder_memory = encoder_memory + from_behind(
            encoder_memory, "section", stride * lane_count
        )
    return encoder_memory


def shards(
    document_token_embedding,
    doc_lengths,
    docid_embed,
    docid_targets,
    enc_gain,
    dec_gain,
    w_enc_qkv,
    w_enc_out,
    cross_query_key_value_weight,
    w_cross_out,
    docid_head_weight,
):
    lane_count = lax.axis_size("section") // GROUPS
    lane_bits = lane_count.bit_length() - 1
    section_index = lax.axis_index("section")
    group_index = section_index // lane_count
    lane_index = section_index % lane_count
    micro_count, row_count, model_width = document_token_embedding.shape
    doc_count = doc_lengths.shape[1]
    doc_span = row_count // doc_count
    block_rows = row_count // lane_count
    local_heads = w_enc_qkv.shape[1] // HD
    positions = jnp.arange(row_count)
    key_doc = positions // doc_span
    key_place = positions % doc_span
    same_doc = key_doc[:, None] == key_doc[None, :]

    def partial_update(normed, lengths):
        allowed = same_doc & live_keys(lengths, key_doc, key_place)[None, :]
        projected = jnp.einsum(
            "rd,mcd->mrc", normed, w_enc_qkv, preferred_element_type=jnp.float32
        ).astype(jnp.bfloat16)
        projected = projected.reshape(3, row_count, local_heads, HD)
        mixture = attend(projected[0], projected[1], projected[2], allowed).reshape(row_count, -1)
        return jnp.dot(mixture, w_enc_out, preferred_element_type=jnp.float32)

    def section_step(step_index, loop_state):
        handed, encoder_memory = loop_state
        micro_index = step_index - group_index
        slot_index = jnp.clip(micro_index, 0, micro_count - 1)
        lengths = lax.dynamic_index_in_dim(doc_lengths, slot_index, 0, keepdims=False)
        layer_gain = lax.dynamic_index_in_dim(enc_gain, group_index, 0, keepdims=False)
        incoming = lax.dynamic_index_in_dim(
            document_token_embedding, jnp.minimum(step_index, micro_count - 1), 0, keepdims=False
        )
        incoming = lax.dynamic_slice_in_dim(incoming, lane_index * block_rows, block_rows, 0)
        current = jnp.where(group_index == 0, incoming, handed)
        normed = lane_gather(
            norm_rows(current, layer_gain).astype(jnp.bfloat16), lane_bits, lane_index, 0
        )
        summed = lane_reduce(partial_update(normed, lengths), lane_bits, lane_index)
        result = (current.astype(jnp.float32) + summed).astype(jnp.bfloat16)
        handed = passed_along(result, "section", lane_count)
        finished_index = step_index - (GROUPS - 1)
        finished_slot = jnp.clip(finished_index, 0, micro_count - 1)
        keeping = (group_index == 0) & (finished_index >= 0) & (finished_index < micro_count)
        stored = lax.dynamic_update_index_in_dim(encoder_memory, handed, finished_slot, 0)
        encoder_memory = jnp.where(keeping, stored, encoder_memory)
        return (handed, encoder_memory)

    handed = jnp.zeros((block_rows, model_width), jnp.bfloat16)
    encoder_memory = jnp.zeros((micro_count, block_rows, model_width), jnp.bfloat16)
    handed, encoder_memory = lax.fori_loop(
        0, micro_count + GROUPS - 1, section_step, (handed, encoder_memory)
    )
    encoder_memory = norm_rows(encoder_memory, enc_gain[GROUPS]).astype(jnp.bfloat16)
    encoder_memory = relay_memory(encoder_memory, group_index, lane_count)
    encoder_memory = lane_gather(encoder_memory, lane_bits, lane_index, 1)
    decoder_rows = docid_embed.shape[1]
    docid_span = decoder_rows // doc_count
    decoder_doc = jnp.arange(decoder_rows) // docid_span
    cross_heads = cross_query_key_value_weight.shape[1] // HD
    dec_normed = norm_rows(docid_embed, dec_gain[0]).astype(jnp.bfloat16)
    queries = jnp.einsum(
        "brd,cd->brc",
        dec_normed,
        cross_query_key_value_weight[0],
        preferred_element_type=jnp.float32,
    ).astype(jnp.bfloat16)
    memory_heads = jnp.einsum(
        "pye,qve->qpyv",
        encoder_memory,
        cross_query_key_value_weight[1:],
        preferred_element_type=jnp.float32,
    ).astype(jnp.bfloat16)

    def cross_one(sample_queries, sample_keys, sample_values, lengths):
        allowed = (decoder_doc[:, None] == key_doc[None, :]) & live_keys(
            lengths, key_doc, key_place
        )[None, :]
        return attend(sample_queries, sample_keys, sample_values, allowed)

    mixture = jax.vmap(cross_one)(
        queries.reshape(micro_count, decoder_rows, cross_heads, HD),
        memory_heads[0].reshape(micro_count, row_count, cross_heads, HD),
        memory_heads[1].reshape(micro_count, row_count, cross_heads, HD),
        doc_lengths,
    )
    cross_terms = jnp.einsum(
        "brc,cd->brd",
        mixture.reshape(micro_count, decoder_rows, -1),
        w_cross_out,
        preferred_element_type=jnp.float32,
    )
    cross_sum = lax.psum(cross_terms, "section")
    closing_rows = norm_rows(docid_embed.astype(jnp.float32) + cross_sum, dec_gain[1]).astype(
        jnp.bfloat16
    )
    scores_vocab = jnp.einsum(
        "brd,dv->brv", closing_rows, docid_head_weight, preferred_element_type=jnp.float32
    )
    vocab_local = docid_head_weight.shape[1]
    vocab_start = section_index * vocab_local
    matches = docid_targets[..., None] == vocab_start + jnp.arange(vocab_local)
    exponent_total, picked = lax.psum(
        (
            jnp.sum(jnp.exp(scores_vocab), axis=-1),
            jnp.sum(jnp.where(matches, scores_vocab, 0.0), axis=-1),
        ),
        "section",
    )
    token_loss = jnp.log(exponent_total) - picked
    mean_loss = lax.psum(jnp.sum(token_loss), "rep") / (token_loss.size * lax.axis_size("rep"))
    return (scores_vocab.astype(jnp.bfloat16), token_loss, mean_loss)


def encoder_kernel(
    sent,
    x_ref,
    gain_ref,
    row_doc_ref,
    key_doc_ref,
    wqkv_ref,
    wout_ref,
    mem_ref,
    wqkv_v,
    wout_v,
    hid,
    work,
    part,
    qkv,
    mix,
    w_sem,
    o_sem,
    x_sem,
    gs,
    gr,
    rs,
    rr,
    zs,
    zr,
    bs,
    br,
    ms,
    mr,
):
    rows, width = hid.shape
    half = sent // 2
    columns = width // PARTS
    tiles = wqkv_v.shape[0]
    per = tiles // 3
    section = lax.axis_index("section")
    count = lax.axis_size("section")
    group = section // 2
    lane = section % 2
    partner = section + 1 - 2 * lane
    ahead = lax.rem(section + 2, count)
    behind = lax.rem(section + count - 2, count)
    own = pl.ds(pl.multiple_of(lane * half, 16), half)
    other = pl.ds(pl.multiple_of((1 - lane) * half, 16), half)

    def cols(c):
        return pl.ds(pl.multiple_of(c * columns, columns), columns)

    def weight_copy(j):
        return pltpu.make_async_copy(
            wqkv_ref.at[j // per, pl.ds((j % per) * WTILE, WTILE)], wqkv_v.at[j], w_sem.at[j]
        )

    def out_copy(c):
        return pltpu.make_async_copy(wout_ref.at[:, cols(c)], wout_v.at[c], o_sem.at[c])

    def remote(src, dst, send, recv, device):
        return pltpu.make_async_remote_copy(
            src_ref=src,
            dst_ref=dst,
            send_sem=send,
            recv_sem=recv,
            device_id={"section": device},
            device_id_type=MESH,
        )

    def gather(c, block):
        return remote(hid.at[block, cols(c)], hid.at[block, cols(c)], gs.at[c], gr.at[c], partner)

    def reduce(c):
        return remote(work.at[other, cols(c)], part.at[:, cols(c)], rs.at[c], rr.at[c], partner)

    def hand(c):
        return remote(hid.at[own, cols(c)], hid.at[own, cols(c)], zs.at[c], zr.at[c], ahead)

    def back(c):
        return remote(mem_ref.at[own, cols(c)], mem_ref.at[own, cols(c)], bs.at[c], br.at[c], behind)

    def spread(c, block):
        return remote(
            mem_ref.at[block, cols(c)], mem_ref.at[block, cols(c)], ms.at[c], mr.at[c], partner
        )

    def each(size, body):
        def step(i, carry):
            body(i)
            return carry

        lax.fori_loop(0, size, step, 0)

    entry = pltpu.make_async_copy(x_ref.at[pl.ds(0, sent)], hid.at[pl.ds(0, sent)], x_sem)

    @pl.when(group == 0)
    def _():
        entry.start()

    for j in range(tiles):
        weight_copy(j).start()
    for c in range(PARTS):
        out_copy(c).start()

    barrier = pltpu.get_barrier_semaphore()
    for device in (partner, ahead, behind):
        pl.semaphore_signal(barrier, inc=1, device_id={"section": device}, device_id_type=MESH)
    pl.semaphore_wait(barrier, 3)

    if sent < rows:
        hid[sent:, :] = jnp.zeros((rows - sent, width), hid.dtype)
    if sent < mem_ref.shape[0]:
        mem_ref[sent:, :] = jnp.zeros((mem_ref.shape[0] - sent, width), mem_ref.dtype)

    @pl.when(group == 0)
    def _():
        entry.wait()

    @pl.when(group > 0)
    def _():
        def arrive(c):
            hand(c).wait_recv()
            gather(c, own).start()

        each(PARTS, arrive)

        def complete(c):
            gather(c, other).wait_recv()
            gather(c, own).wait_send()

        each(PARTS, complete)

    def norm(r):
        block = pl.ds(pl.multiple_of(r * 16, 16), 16)
        values = hid[block, :].astype(jnp.float32)
        scale = lax.rsqrt(jnp.mean(values * values, axis=-1, keepdims=True) + 1e-06)
        work[block, :] = (values * scale * gain_ref[...]).astype(work.dtype)

    each(rows // 16, norm)

    def project(j):
        pltpu.make_async_copy(
            wqkv_ref.at[0, pl.ds(0, WTILE)], wqkv_v.at[j], w_sem.at[j]
        ).wait()
        qkv[j] = lax.dot_general(
            work[...], wqkv_v[j], (((1,), (1,)), ((), ())), preferred_element_type=jnp.float32
        ).astype(qkv.dtype)

    each(tiles, project)
    pairs = WTILE // (2 * HD)

    def attend_pair(p):
        tile = p // pairs
        span = pl.ds(pl.multiple_of((p % pairs) * 2 * HD, 2 * HD), 2 * HD)
        queries = qkv[tile, :, span]
        keys = qkv[per + tile, :, span]
        values = qkv[2 * per + tile, :, span]
        allowed = row_doc_ref[...] == key_doc_ref[...]
        first = lax.broadcasted_iota(jnp.int32, (rows, 2 * HD), 1) < HD
        mixed = []
        for side in range(2):
            keep = first if side == 0 else jnp.logical_not(first)
            chosen = jnp.where(keep, queries.astype(jnp.float32), 0.0).astype(jnp.bfloat16)
            scores = lax.dot_general(
                chosen, keys, (((1,), (1,)), ((), ())), preferred_element_type=jnp.float32
            )
            weights = jnp.where(allowed, jnp.exp(scores), 0.0)
            shares = (weights / jnp.sum(weights, axis=-1, keepdims=True)).astype(jnp.bfloat16)
            mixed.append(jnp.dot(shares, values, preferred_element_type=jnp.float32))
        mix[:, pl.ds(pl.multiple_of(p * 2 * HD, 2 * HD), 2 * HD)] = jnp.where(
            first, mixed[0], mixed[1]
        ).astype(mix.dtype)

    each(per * pairs, attend_pair)

    def output(c):
        out_copy(c).wait()
        work[:, cols(c)] = jnp.dot(
            mix[...], wout_v[c], preferred_element_type=jnp.float32
        ).astype(work.dtype)
        reduce(c).start()

    each(PARTS, output)

    def total(c):
        reduce(c).wait_recv()
        return (
            hid[own, cols(c)].astype(jnp.float32)
            + work[own, cols(c)].astype(jnp.float32)
            + part[:, cols(c)].astype(jnp.float32)
        ).astype(hid.dtype)

    @pl.when(group < GROUPS - 1)
    def _():
        def finish(c):
            hid[own, cols(c)] = total(c)
            hand(c).start()

        each(PARTS, finish)

        def relay(c):
            back(c).wait_recv()

            @pl.when(group > 0)
            def _():
                back(c).start()

            spread(c, own).start()

        each(PARTS, relay)

    @pl.when(group == GROUPS - 1)
    def _():
        def finish(c):
            mem_ref[own, cols(c)] = total(c)
            back(c).start()
            spread(c, own).start()

        each(PARTS, finish)

    def drain(c):
        spread(c, other).wait_recv()
        spread(c, own).wait_send()
        reduce(c).wait_send()

        @pl.when(group < GROUPS - 1)
        def _():
            hand(c).wait_send()

        @pl.when(group > 0)
        def _():
            back(c).wait_send()

    each(PARTS, drain)


def encode(rows, sent, number, x, gain, row_doc, key_doc, wqkv, wout):
    total_rows, width = x.shape
    inner = wout.shape[0]
    tiles = 3 * (inner // WTILE)
    dma = pltpu.SemaphoreType.DMA
    vmem = pl.BlockSpec(memory_space=pltpu.VMEM)
    anywhere = pl.BlockSpec(memory_space=pl.ANY)
    return pl.pallas_call(
        functools.partial(encoder_kernel, sent),
        out_shape=jax.ShapeDtypeStruct((total_rows, width), jnp.bfloat16),
        in_specs=[anywhere, vmem, vmem, vmem, anywhere, anywhere],
        out_specs=vmem,
        scratch_shapes=[
            pltpu.VMEM((tiles, WTILE, width), jnp.bfloat16),
            pltpu.VMEM((PARTS, inner, width // PARTS), jnp.bfloat16),
            pltpu.VMEM((rows, width), jnp.bfloat16),
            pltpu.VMEM((rows, width), jnp.bfloat16),
            pltpu.VMEM((sent // 2, width), jnp.bfloat16),
            pltpu.VMEM((tiles, rows, WTILE), jnp.bfloat16),
            pltpu.VMEM((rows, inner), jnp.bfloat16),
            dma((tiles,)),
            dma((PARTS,)),
            dma,
        ]
        + [dma((PARTS,))] * 10,
        compiler_params=pltpu.CompilerParams(
            collective_id=number, has_side_effects=True, vmem_limit_bytes=67043328
        ),
        name=f"encoder_{sent}",
    )(x, gain, row_doc[:rows, None], key_doc[None, :rows], wqkv, wout)


def butterfly(value, axis, combine):
    for bit in range(lax.axis_size(axis).bit_length() - 1):
        value = combine(value, from_partner(value, axis, bit))
    return value


def greet(me, count):
    barrier = pltpu.get_barrier_semaphore()
    for k in range(1, count):
        pl.semaphore_signal(
            barrier, inc=1, device_id={"section": lax.rem(me + k, count)}, device_id_type=MESH
        )
    pl.semaphore_wait(barrier, count - 1)


def to_peer(src, dst, send, recv, peer):
    return pltpu.make_async_remote_copy(
        src_ref=src,
        dst_ref=dst,
        send_sem=send,
        recv_sem=recv,
        device_id={"section": peer},
        device_id_type=MESH,
    )


def closing_kernel(terms, residual, gain, out, landed, s1, r1, s2, r2):
    count = terms.shape[0]
    me = lax.axis_index("section")
    greet(me, count)

    def scatter(k, slot):
        peer = lax.rem(me + k, count)
        return to_peer(terms.at[peer], landed.at[slot], s1.at[k], r1.at[k], peer)

    def gather(k, slot):
        return to_peer(out.at[slot], out.at[slot], s2.at[k], r2.at[k], lax.rem(me + k, count))

    for k in range(1, count):
        scatter(k, me).start()
    total = residual[...] + terms[me].astype(jnp.float32)
    for k in range(1, count):
        slot = lax.rem(me + count - k, count)
        scatter(k, slot).wait_recv()
        total = total + landed[slot].astype(jnp.float32)
    scale = lax.rsqrt(jnp.mean(total * total, axis=-1, keepdims=True) + 1e-06)
    out[me] = (total * scale * gain[...]).astype(out.dtype)
    for k in range(1, count):
        gather(k, me).start()
    for k in range(1, count):
        gather(k, lax.rem(me + count - k, count)).wait_recv()
    for k in range(1, count):
        scatter(k, me).wait_send()
        gather(k, me).wait_send()


def closing_rows_of(terms, residual, gain):
    count = terms.shape[0]
    dma = pltpu.SemaphoreType.DMA
    vmem = pl.BlockSpec(memory_space=pltpu.VMEM)
    return pl.pallas_call(
        closing_kernel,
        out_shape=jax.ShapeDtypeStruct(terms.shape, jnp.bfloat16),
        in_specs=[vmem] * 3,
        out_specs=vmem,
        scratch_shapes=[pltpu.VMEM(terms.shape, jnp.bfloat16)] + [dma((count,))] * 4,
        compiler_params=pltpu.CompilerParams(collective_id=8, has_side_effects=True),
        name="closing",
    )(terms, residual, gain)


def sums_kernel(value, out, landed, send, recv):
    count = landed.shape[0]
    me = lax.axis_index("section")
    greet(me, count)

    def share(k, slot):
        return to_peer(value, landed.at[slot], send.at[k], recv.at[k], lax.rem(me + k, count))

    for k in range(1, count):
        share(k, me).start()
    landed[me] = value[...]
    for k in range(1, count):
        share(k, lax.rem(me + count - k, count)).wait_recv()
    total = landed[0]
    for k in range(1, count):
        total = total + landed[k]
    out[...] = total
    for k in range(1, count):
        share(k, me).wait_send()


def section_sum(value, count):
    dma = pltpu.SemaphoreType.DMA
    vmem = pl.BlockSpec(memory_space=pltpu.VMEM)
    return pl.pallas_call(
        sums_kernel,
        out_shape=jax.ShapeDtypeStruct(value.shape, value.dtype),
        in_specs=[vmem],
        out_specs=vmem,
        scratch_shapes=[pltpu.VMEM((count,) + value.shape, value.dtype)] + [dma((count,))] * 2,
        compiler_params=pltpu.CompilerParams(collective_id=9, has_side_effects=True),
        name="section_sum",
    )(value)


def fast_shards(
    document_token_embedding,
    doc_lengths,
    docid_embed,
    docid_targets,
    enc_gain,
    dec_gain,
    w_enc_qkv,
    w_enc_out,
    cross_query_key_value_weight,
    w_cross_out,
    docid_head_weight,
):
    section_index = lax.axis_index("section")
    group_index = section_index // 2
    micro_count, row_count, width = document_token_embedding.shape
    doc_count = doc_lengths.shape[1]
    doc_span = row_count // doc_count
    all_rows = micro_count * row_count
    positions = jnp.arange(all_rows)
    lengths = doc_lengths.reshape(-1)
    live = (jnp.arange(doc_span)[None, :] < lengths[:, None]).reshape(-1)
    ends = jnp.cumsum(lengths)
    live_count = ends[-1]
    starts = jnp.concatenate([jnp.zeros((1,), ends.dtype), ends[:-1]])
    inside = (positions[:, None] >= starts[None, :]) & (positions[:, None] < ends[None, :])
    docs = jnp.arange(lengths.shape[0])
    row_doc = jnp.sum(jnp.where(inside, docs[None, :], 0), axis=1).astype(jnp.int32)
    key_doc = jnp.where(positions < live_count, row_doc, -1).astype(jnp.int32)
    source = jnp.sum(
        jnp.where(inside, docs[None, :] * doc_span + positions[:, None] - starts[None, :], 0), axis=1
    )
    source = jnp.where(positions < live_count, source, -1)
    pick = (source[:, None] == positions[None, :]).astype(jnp.bfloat16)
    packed = jnp.dot(
        pick,
        document_token_embedding.reshape(all_rows, width),
        preferred_element_type=jnp.float32,
    ).astype(jnp.bfloat16)
    largest = butterfly(live_count.astype(jnp.float32)[None], "rep", jnp.maximum)[0]
    gain = lax.dynamic_slice_in_dim(enc_gain, group_index, 1, 0)
    unit = all_rows // 2
    sizes = [(unit, unit * 3 // 4), (unit, unit), (all_rows, all_rows)]
    choice = jnp.sum(jnp.stack([(largest > sent).astype(jnp.int32) for _, sent in sizes[:-1]]))
    branches = [
        functools.partial(encode, rows, sent, number) for number, (rows, sent) in enumerate(sizes)
    ]
    hidden = lax.switch(
        choice, branches, packed, gain, row_doc, key_doc, w_enc_qkv, w_enc_out
    )
    memory = norm_rows(hidden, enc_gain[GROUPS]).astype(jnp.bfloat16)

    decoder_rows = docid_embed.shape[1]
    every = micro_count * decoder_rows
    docid_span = decoder_rows // doc_count
    decoder_doc = jnp.arange(every) // docid_span
    cross_heads = cross_query_key_value_weight.shape[1] // HD
    flat_docid = docid_embed.reshape(every, width)
    dec_normed = norm_rows(flat_docid, dec_gain[0]).astype(jnp.bfloat16)

    def project(values, weight):
        return (
            jnp.einsum("rd,cd->rc", values, weight, preferred_element_type=jnp.float32)
            .astype(jnp.bfloat16)
            .reshape(-1, cross_heads, HD)
        )

    queries = project(dec_normed, cross_query_key_value_weight[0])
    keys = project(memory, cross_query_key_value_weight[1])
    values = project(memory, cross_query_key_value_weight[2])
    allowed = decoder_doc[:, None] == key_doc[None, :]
    mixture = attend(queries, keys, values, allowed).reshape(every, -1)
    cross_terms = jnp.dot(mixture, w_cross_out, preferred_element_type=jnp.float32)
    section_count = lax.axis_size("section")
    share = every // section_count
    residual = lax.dynamic_slice_in_dim(flat_docid, section_index * share, share, 0)
    closing = closing_rows_of(
        cross_terms.astype(jnp.bfloat16).reshape(section_count, share, width),
        residual.astype(jnp.float32),
        dec_gain[1:2],
    ).reshape(every, width)
    scores_vocab = jnp.dot(closing, docid_head_weight, preferred_element_type=jnp.float32)
    vocab_local = docid_head_weight.shape[1]
    targets = docid_targets.reshape(-1)
    matches = targets[:, None] == section_index * vocab_local + jnp.arange(vocab_local)
    sums = jnp.stack(
        [
            jnp.sum(jnp.exp(scores_vocab), axis=-1),
            jnp.sum(jnp.where(matches, scores_vocab, 0.0), axis=-1),
        ]
    )
    padding = ((0, -sums.shape[0] % 8), (0, -sums.shape[1] % 128))
    sums = section_sum(jnp.pad(sums, padding), section_count)[:2, :every]
    token_loss = jnp.log(sums[0]) - sums[1]
    loss_sum = butterfly(jnp.sum(token_loss)[None], "rep", jnp.add)[0]
    mean_loss = loss_sum / (token_loss.size * lax.axis_size("rep"))
    logits = scores_vocab.astype(jnp.bfloat16).reshape(micro_count, decoder_rows, vocab_local)
    return (logits, token_loss.reshape(docid_targets.shape), mean_loss)


def solution(mesh):
    in_specs = (
        P("rep", None, None),
        P("rep", None),
        P("rep", None, None),
        P("rep", None),
        P(),
        P(),
        P(None, "section", None),
        P("section", None),
        P(None, "section", None),
        P("section", None),
        P(None, "section"),
    )
    out_specs = (P("rep", None, "section"), P("rep", None), P())
    local = shards if mesh.shape["section"] != 2 * GROUPS else fast_shards
    return jax.shard_map(local, mesh=mesh, in_specs=in_specs, out_specs=out_specs, check_vma=False)
```
